1024 devices in a mesh: pipe: 16 (over z), expert: 64 (over x, y, core).
Axes of the slice: x: 4, y: 8, z: 16, core: 2. Of those that a mesh axis runs over, the one named last changes fastest.
Arguments:
- up_state: bfloat16 [16, 2048, 3584], P('pipe', 'expert'), may hold values from -6 to 6
- down_state: bfloat16 [16, 2048, 3584], P('pipe', 'expert'), may hold values from -6 to 6
- entering: bfloat16 [2, 1, 2048, 3584], P(None, None, 'expert'), may hold values from -6 to 6
- norm_gain: float32 [16, 3584], P('pipe'), may hold values from 0.1 to 1.9
- router: bfloat16 [16, 3584, 32], P('pipe'), may hold values from -0.09375 to 0.09375
- routes: int32 [16, 2, 64, 64, 1], P('pipe', None, 'expert'), may hold values from 0 to 31; in each aligned block of 64 rows (0 to 63, 64 to 127, ..., all dimensions but the last counted through in order) at most 4 rows name the same one
- w_in: bfloat16 [3584, 32768], P(None, 'expert'), may hold values from -0.09375 to 0.09375
- w_out: bfloat16 [32768, 3584], P('expert'), may hold values from -0.1875 to 0.1875
Outputs:
- up_out: bfloat16 [16, 2048, 3584], P('pipe', 'expert')
- down_out: bfloat16 [16, 2048, 3584], P('pipe', 'expert')
The draws below stay inside these ranges and needn't reach their ends.
Inputs may be any that keep to these rules, and one draw needn't show every extreme that they name: `routes`: the 1 ids of a row are distinct. Among the 64 rows of one index of expert at one section and step, no expert is chosen more than 4 times, and some expert is chosen exactly 4 times.
All inputs are finite; a program needn't handle non-finite values.
Results may differ from the reference program's by a relative error of at most 0.0067.
Values may be sent and summed in bfloat16 or wider, within the bound.
A program may use at most 32 MiB of HBM per device.

```python
import math
import jax
import jax.numpy as jnp
import numpy as np
from jax import lax

D = 3584
FF = 1024
HOLDERS = 2
TOPK = 1
STEPS = 2
TOK = 32
EXPERTS = 32
TOKENS = 2048
CAP = 4
N_PIPE = 16
N_EXPERT = 64


def levels(own_key, extent, shards, least, top_value):
    def one(axis_at, shards_of):
        draws = jax.random.uniform(jax.random.fold_in(jax.random.fold_in(own_key, 6), axis_at), (shards_of,), jnp.float32, least / len(shards), top_value / len(shards))
        return jnp.repeat(jnp.exp(draws), extent[axis_at] // shards_of).reshape((-1,) + (1,) * (len(extent) - axis_at - 1))

    level = one(*shards[0])
    for cut in shards[1:]:
        level = level * one(*cut)
    return level


def routed_block(key, own, number, rows, amount, top, bound, lean):
    sequence = jax.random.permutation(key, amount)
    packed, common = portions_of(amount, rows * top, bound, lean, True), portions_of(amount, rows * top, bound, lean, False)
    places = jnp.arange(amount)

    def named(sizes, offset_by):
        used = int((sizes > 0).sum())
        fixed = max(1, used // 4)
        moved = fixed + (places - fixed + offset_by * (used - fixed)) % max(1, amount - fixed)
        return jnp.zeros((amount,), jnp.int32).at[sequence[jnp.where(places < fixed, places, moved)]].set(jnp.asarray(sizes, jnp.int32))

    sizes = jnp.where(number % 4 == 0, named(packed, number // 4), named(common, number - number // 4 - 1))
    mixed = jax.random.permutation(jax.random.fold_in(own, 3), amount)
    giver, taker = mixed[0:amount // 2 * 2:2], mixed[1:amount // 2 * 2:2]
    margin = jnp.minimum(sizes[giver] - 1, bound - sizes[taker]) // 2
    margin = jnp.where((giver == sequence[0]) | (taker == sequence[0]) | (sizes[taker] == 0), 0, jnp.maximum(margin, 0))
    moved = jax.random.randint(jax.random.fold_in(own, 4), (amount // 2,), 0, 1 << 20) % (margin + 1)
    sizes = sizes.at[giver].add(-moved).at[taker].add(moved)
    members = jnp.searchsorted(jnp.cumsum(sizes), jnp.arange(rows * top), side="right").astype(jnp.int32)
    grid = members.reshape(top, rows).T
    grid = grid[jax.random.permutation(jax.random.fold_in(own, 1), rows)]
    offset_by = jax.random.randint(jax.random.fold_in(own, 2), (rows, 1), 0, top)
    return jnp.take_along_axis(grid, (jnp.arange(top)[None, :] + offset_by) % top, axis=1)


def portions_of(number_of, total, most, slope, full):
    portions = [(1 << 20) // math.isqrt(grade ** slope) + 1 for grade in range(1, number_of + 1)]
    largest = most if full else min(most, max(-(-total // number_of), total * portions[0] // sum(portions)))
    least = 1 if total - largest >= number_of - 1 else 0
    given, surplus = [largest] + [least] * (number_of - 1), total - largest - least * (number_of - 1)
    while surplus > 0:
        candidates = [i for i in range(1, number_of) if given[i] < largest] or [i for i in range(1, number_of) if given[i] < most]
        whole, left = sum([portions[i] for i in candidates]), surplus
        for i in candidates:
            addition = min(most - given[i], max(1, left * portions[i] // whole), surplus)
            given[i] = given[i] + addition
            surplus = surplus - addition
    return np.array(given)


def gaussian(key, dims, scale, bound, cuts=(), kind=jnp.bfloat16):
    loudness = levels(key, dims, cuts, -0.22, 0.18) if cuts else 1.0
    array = jax.random.normal(key, dims, jnp.float32) * scale * loudness
    return jnp.minimum(jnp.maximum(array, -bound), bound).astype(kind)


def setup_inputs(seed: int = 0) -> dict:
    keys = jax.random.split(jax.random.key(seed), 9)
    up_state = gaussian(keys[0], (N_PIPE, TOKENS, D), 1.0, 6.0, ((0, 16), (1, 64)))
    down_state = gaussian(keys[1], (N_PIPE, TOKENS, D), 1.0, 6.0, ((0, 16), (1, 64)))
    entering = gaussian(keys[2], (2, STEPS - 1, TOKENS, D), 1.0, 6.0, ((2, 64),))
    norm_gain = jnp.clip(1.0 + 0.18 * jax.random.normal(keys[3], (N_PIPE, D), jnp.float32), 0.1, 1.9)
    router = gaussian(keys[4], (N_PIPE, D, EXPERTS), D ** -0.5, 0.09375, ((0, 16),))
    routes_keys = jax.random.split(jax.random.fold_in(keys[5], 1), N_PIPE * STEPS * N_EXPERT * (2 * TOK) // (2 * TOK))
    routes_turns = jax.random.permutation(jax.random.fold_in(keys[5], 3), N_PIPE * STEPS * N_EXPERT * (2 * TOK) // (2 * TOK))
    routes = jax.vmap(lambda own, number: routed_block(jax.random.fold_in(keys[5], 2), own, number, 2 * TOK, EXPERTS, TOPK, CAP, 2))(routes_keys, routes_turns).reshape((N_PIPE, STEPS, N_EXPERT, 2 * TOK, TOPK))
    w_in = gaussian(keys[6], (D, EXPERTS * FF), D ** -0.5, 0.09375, ((1, 64),))
    w_out = gaussian(keys[7], (EXPERTS * FF, D), FF ** -0.5, 0.1875, ((0, 64),))
    return dict(up_state=up_state, down_state=down_state, entering=entering, norm_gain=norm_gain, router=router, routes=routes, w_in=w_in, w_out=w_out)


ROUTE_SCALE = 2.5
NORM_EPS = 1e-06

def normalize(row_block, gain_row):
    values = row_block.astype(jnp.float32)
    square = lax.optimization_barrier(jnp.mean(values * values, axis=-1, keepdims=True))
    return (values * lax.rsqrt(square + NORM_EPS) * gain_row).astype(jnp.bfloat16)

def section_layer(up_rows, down_rows, gain_row, router_cols, step_ids, w_in, w_out):
    width = up_rows.shape[1]
    row_block = jnp.concatenate([up_rows.reshape(N_EXPERT, TOK, width), down_rows.reshape(N_EXPERT, TOK, width)], axis=1).reshape(N_EXPERT * 2 * TOK, width)
    flat_ids = step_ids.reshape(N_EXPERT * 2 * TOK, TOPK).astype(jnp.int32)
    normed = normalize(row_block, gain_row)
    scores = jax.nn.sigmoid(jnp.dot(normed, router_cols, preferred_element_type=jnp.float32))
    gate_items = (ROUTE_SCALE * jnp.take_along_axis(scores, flat_ids, axis=1)).reshape(-1)
    item_ids = flat_ids.reshape(-1)
    piece_count = item_ids.shape[0]
    slot_count = N_EXPERT * CAP
    half_units = FF // HOLDERS

    def one_expert(expert_num):
        is_member = (item_ids == expert_num).astype(jnp.int32)
        position = (jnp.cumsum(is_member) - 1).astype(jnp.int32)
        target = jnp.where(is_member > 0, position, slot_count).astype(jnp.int32)
        picked = jnp.zeros((slot_count,), jnp.int32).at[target].set(jnp.arange(piece_count, dtype=jnp.int32), mode='drop')
        live_count = jnp.sum(is_member).astype(jnp.int32)
        live_slot = jnp.arange(slot_count, dtype=jnp.int32) < live_count
        chosen = jnp.where(live_slot[:, None], normed[picked // TOPK], jnp.zeros((), normed.dtype))
        col_start = (expert_num * FF).astype(jnp.int32)
        in_cols = lax.dynamic_slice_in_dim(w_in, col_start, FF, 1)
        out_rows = lax.dynamic_slice_in_dim(w_out, col_start, FF, 0)
        hidden = jax.nn.silu(jnp.dot(chosen, in_cols, preferred_element_type=jnp.float32)).astype(jnp.bfloat16)
        first_part = jnp.dot(hidden[:, :half_units], out_rows[:half_units], preferred_element_type=jnp.float32).astype(jnp.bfloat16)
        second_part = jnp.dot(hidden[:, half_units:], out_rows[half_units:], preferred_element_type=jnp.float32).astype(jnp.bfloat16)
        first_part = lax.optimization_barrier(first_part)
        second_part = lax.optimization_barrier(second_part)
        expert_out = first_part.astype(jnp.float32) + second_part.astype(jnp.float32)
        weight = jnp.where(live_slot, gate_items[picked], 0.0)
        return (picked, expert_out * weight[:, None])
    all_picks, expert_parts = lax.map(one_expert, jnp.arange(EXPERTS, dtype=jnp.int32))
    moe_total = jnp.zeros((row_block.shape[0], width), jnp.float32).at[(all_picks // TOPK).reshape(-1)].add(expert_parts.reshape(-1, width))
    advanced = (row_block.astype(jnp.float32) + moe_total).astype(jnp.bfloat16).reshape(N_EXPERT, 2 * TOK, width)
    return (advanced[:, :TOK].reshape(TOKENS, width), advanced[:, TOK:].reshape(TOKENS, width))

def reference(up_state, down_state, entering, norm_gain, router, routes, w_in, w_out):

    def one_section(pieces):
        return section_layer(pieces[0], pieces[1], pieces[2], pieces[3], pieces[4], w_in, w_out)
    upward = up_state
    downward = down_state
    up_new = up_state
    down_new = down_state
    for step_idx in range(STEPS):
        up_new, down_new = lax.map(one_section, (upward, downward, norm_gain, router, routes[:, step_idx]))
        if step_idx + 1 < STEPS:
            upward = jnp.concatenate([entering[0, step_idx][None], up_new[:-1]], axis=0)
            downward = jnp.concatenate([down_new[1:], entering[1, step_idx][None]], axis=0)
    return (up_new, down_new)
```

```python
import functools

import jax
import jax.numpy as jnp
from jax import lax
from jax.experimental import pallas as pl
from jax.experimental.pallas import tpu as pltpu
from jax.sharding import PartitionSpec as P

STEPS = 2
ROUTE_SCALE = 2.5
NORM_EPS = 1e-06

NX, NY = 4, 8
CHIPS = NX * NY
CAP = 4
CHUNK = 512
GROUPS = 2
LAG = 2
MESH = pl.DeviceIdType.MESH
BF16 = jnp.bfloat16
F32 = jnp.float32

OFFSETS = [(dx, dy) for dx in range(NX) for dy in range(NY)]


def hops(offset):
    return min(offset[0], NX - offset[0]) + min(offset[1], NY - offset[1])


def window_kernel(
    up_ref, down_ref, entering_ref, gain_ref, router_ref, routes_ref, w_in_ref, w_out_ref,
    up_out, down_out,
    w_in, w_out, rows, sent, got, made, back, hop_sent, hop_got, acc, hidden, spare,
    in_sem, out_sem, wsend_sem, sent_sem, got_sem, made_sem, back_sem, hop_send_sem, hop_sem,
):
    tok, width = up_ref.shape
    row_count = 2 * tok
    chunks = width // CHUNK
    slots = CHIPS * CAP
    group_rows = slots // GROUPS
    group_offsets = CHIPS // GROUPS

    section = lax.axis_index("pipe")
    last_section = lax.axis_size("pipe") - 1
    place = lax.axis_index("expert")
    core = place % 2
    chip_x = (place // 2) // NY
    chip_y = (place // 2) % NY
    partner = place + 1 - 2 * core
    above = lax.rem(section + 1, last_section + 1)
    below = lax.rem(section + last_section, last_section + 1)

    def peer(dx, dy, sign):
        x = (chip_x + sign * dx + NX) % NX
        y = (chip_y + sign * dy + NY) % NY
        return (x * NY + y) * 2 + core

    def columns(c):
        return pl.ds(pl.multiple_of(c * CHUNK, CHUNK), CHUNK)

    def local_weights(c, _):
        pltpu.make_async_copy(w_in_ref.at[columns(c)], w_in.at[core, columns(c)], in_sem.at[c]).start()
        pltpu.make_async_copy(
            w_out_ref.at[:, columns(c)], w_out.at[core, :, columns(c)], out_sem.at[c]
        ).start()
        return 0

    lax.fori_loop(0, chunks, local_weights, 0)

    barrier = pltpu.get_barrier_semaphore()
    for dx, dy in sorted(OFFSETS[1:], key=hops, reverse=True):
        pl.semaphore_signal(
            barrier, inc=1, device_id={"expert": peer(dx, dy, 1)}, device_id_type=MESH
        )
    for target in (above, below):
        pl.semaphore_signal(barrier, inc=1, device_id={"pipe": target}, device_id_type=MESH)
    pl.semaphore_signal(barrier, inc=1, device_id={"expert": partner}, device_id_type=MESH)

    def route(step):
        ids = routes_ref[step]
        member = (
            ids == lax.broadcasted_iota(jnp.int32, (row_count, CHIPS), 1)
        ).astype(F32)
        earlier = (
            lax.broadcasted_iota(jnp.int32, (row_count, row_count), 1)
            < lax.broadcasted_iota(jnp.int32, (row_count, row_count), 0)
        ).astype(F32)
        ranks = jnp.dot(earlier.astype(BF16), member.astype(BF16), preferred_element_type=F32)
        rank = jnp.sum(ranks * member, axis=1, keepdims=True).astype(jnp.int32)
        far_x = (lax.div(ids, NY) - chip_x + NX) & (NX - 1)
        far_y = ((ids & (NY - 1)) - chip_y + NY) & (NY - 1)
        slot = (far_x * NY + far_y) * CAP + rank
        place_row = (slot == lax.broadcasted_iota(jnp.int32, (row_count, slots), 1)).astype(F32)
        return member, place_row.astype(BF16), jnp.transpose(place_row).astype(BF16)

    plans = [route(step) for step in range(STEPS)]

    def admit(step, c, carry, chunk_rows):
        square, scores = carry
        rows[step, c] = chunk_rows
        values = chunk_rows.astype(F32)
        square = square + jnp.sum(values * values, axis=1, keepdims=True)
        scaled = (values * gain_ref[:, columns(c)]).astype(BF16)
        scores = scores + jnp.dot(scaled, router_ref[columns(c)], preferred_element_type=F32)
        sent[step, c] = jnp.dot(plans[step][2], chunk_rows, preferred_element_type=F32).astype(BF16)
        return square, scores

    def dispatch(step, group, c):
        for k in range(group * group_offsets, (group + 1) * group_offsets):
            mine = sent.at[step, c, pl.ds(CAP * k, CAP)]
            theirs = got.at[step, c, pl.ds(CAP * k, CAP)]
            if k == 0:
                pltpu.make_async_copy(mine, theirs, got_sem.at[step, group, c]).start()
                pltpu.make_async_copy(
                    mine, spare.at[2 * step, c, pl.ds(0, CAP)], sent_sem.at[step]
                ).start()
                continue
            pltpu.make_async_remote_copy(
                src_ref=mine,
                dst_ref=theirs,
                send_sem=sent_sem.at[step],
                recv_sem=got_sem.at[step, group, c],
                device_id={"expert": peer(*OFFSETS[k], 1)},
                device_id_type=MESH,
            ).start()

    def give_back(step, group, c):
        for k in range(group * group_offsets, (group + 1) * group_offsets):
            mine = made.at[step, c, pl.ds(CAP * k, CAP)]
            theirs = back.at[step, c, pl.ds(CAP * k, CAP)]
            if k == 0:
                pltpu.make_async_copy(mine, theirs, back_sem.at[step, group, c]).start()
                pltpu.make_async_copy(
                    mine, spare.at[2 * step + 1, c, pl.ds(0, CAP)], made_sem.at[step]
                ).start()
                continue
            pltpu.make_async_remote_copy(
                src_ref=mine,
                dst_ref=theirs,
                send_sem=made_sem.at[step],
                recv_sem=back_sem.at[step, group, c],
                device_id={"expert": peer(*OFFSETS[k], -1)},
                device_id_type=MESH,
            ).start()

    def wait_bytes(ref, sem):
        pltpu.make_async_copy(ref, ref, sem).wait()

    def experts(step, group):
        own = pl.ds(group * group_rows, group_rows)
        acc[...] = jnp.zeros_like(acc)

        def enter(c, square):
            wait_bytes(got.at[step, c, own], got_sem.at[step, group, c])
            if step == 0 and group == 0:
                wait_bytes(w_in.at[:, columns(c)], in_sem.at[c])
            values = got[step, c, own].astype(F32)
            square = square + jnp.sum(values * values, axis=1, keepdims=True)
            scaled = (values * gain_ref[:, columns(c)]).astype(BF16)
            for half in range(2):
                acc[half] += jnp.dot(scaled, w_in[half, columns(c)], preferred_element_type=F32)
            return square

        square = lax.fori_loop(0, chunks, enter, jnp.zeros((group_rows, 1), F32))
        factor = lax.rsqrt(square * (1.0 / width) + NORM_EPS)
        for half in range(2):
            hidden[half] = jax.nn.silu(acc[half] * factor).astype(BF16)

        def leave(c, _):
            if step == 0 and group == 0:
                wait_bytes(w_out.at[:, :, columns(c)], out_sem.at[c])
            total = jnp.dot(hidden[0], w_out[0, :, columns(c)], preferred_element_type=F32)
            total += jnp.dot(hidden[1], w_out[1, :, columns(c)], preferred_element_type=F32)
            made[step, c, own] = total.astype(BF16)
            give_back(step, group, c)
            return 0

        lax.fori_loop(0, chunks, leave, 0)

    def gate_of(step, carry):
        square, scores = carry
        factor = lax.rsqrt(square * (1.0 / width) + NORM_EPS)
        weights = jax.nn.sigmoid(scores * factor)
        return ROUTE_SCALE * jnp.sum(weights * plans[step][0], axis=1, keepdims=True)

    def combine(step, c, gate):
        for group in range(GROUPS):
            own = pl.ds(group * group_rows, group_rows)
            wait_bytes(back.at[step, c, own], back_sem.at[step, group, c])
        chosen = jnp.dot(plans[step][1], back[step, c], preferred_element_type=F32)
        return (rows[step, c].astype(F32) + gate * chosen).astype(BF16)

    empty = (jnp.zeros((row_count, 1), F32), jnp.zeros((row_count, CHIPS), F32))

    def first_rows(c, carry):
        chunk_rows = jnp.concatenate([up_ref[:, columns(c)], down_ref[:, columns(c)]], axis=0)
        return admit(0, c, carry, chunk_rows)

    carry = lax.fori_loop(0, chunks, first_rows, empty)

    pl.semaphore_wait(barrier, CHIPS + 2)

    def push_in(c, _):
        pltpu.make_async_remote_copy(
            src_ref=w_in_ref.at[columns(c)],
            dst_ref=w_in.at[core, columns(c)],
            send_sem=wsend_sem.at[0],
            recv_sem=in_sem.at[c],
            device_id={"expert": partner},
            device_id_type=MESH,
        ).start()
        return 0

    def push_out(c, _):
        pltpu.make_async_remote_copy(
            src_ref=w_out_ref.at[:, columns(c)],
            dst_ref=w_out.at[core, :, columns(c)],
            send_sem=wsend_sem.at[1],
            recv_sem=out_sem.at[c],
            device_id={"expert": partner},
            device_id_type=MESH,
        ).start()
        return 0

    def send_group(step, group):
        def one(c, _):
            dispatch(step, group, c)
            return 0

        lax.fori_loop(0, chunks, one, 0)

    send_group(0, 0)
    lax.fori_loop(0, chunks, push_in, 0)
    send_group(0, 1)
    lax.fori_loop(0, chunks, push_out, 0)

    for step in range(STEPS):
        gate = gate_of(step, carry)
        for group in range(GROUPS):
            experts(step, group)
        if step + 1 < STEPS:

            def relay(c):
                hop_sent[step, c] = combine(step, c, gate)
                for half, target in ((0, above), (1, below)):
                    part = pl.ds(half * tok, tok)
                    pltpu.make_async_remote_copy(
                        src_ref=hop_sent.at[step, c, part],
                        dst_ref=hop_got.at[step, c, part],
                        send_sem=hop_send_sem.at[step],
                        recv_sem=hop_sem.at[step, c],
                        device_id={"pipe": target},
                        device_id_type=MESH,
                    ).start()

            def take(c, carry):
                wait_bytes(hop_got.at[step, c], hop_sem.at[step, c])
                upward = jnp.where(
                    section == 0, entering_ref[0, step, :, columns(c)], hop_got[step, c, pl.ds(0, tok)]
                )
                downward = jnp.where(
                    section == last_section,
                    entering_ref[1, step, :, columns(c)],
                    hop_got[step, c, pl.ds(tok, tok)],
                )
                carry = admit(step + 1, c, carry, jnp.concatenate([upward, downward], axis=0))
                dispatch(step + 1, 0, c)
                return carry

            def head(c, _):
                relay(c)
                return 0

            def middle(c, carry):
                relay(c)
                return take(c - LAG, carry)

            lax.fori_loop(0, LAG, head, 0)
            carry = lax.fori_loop(LAG, chunks, middle, empty)
            carry = lax.fori_loop(chunks - LAG, chunks, take, carry)
            for group in range(1, GROUPS):
                send_group(step + 1, group)
        else:

            def finish(c, _):
                result = combine(step, c, gate)
                up_out[:, columns(c)] = result[:tok]
                down_out[:, columns(c)] = result[tok:]
                return 0

            lax.fori_loop(0, chunks, finish, 0)

    for step in range(STEPS):
        wait_bytes(sent.at[step], sent_sem.at[step])
        wait_bytes(made.at[step], made_sem.at[step])
        if step + 1 < STEPS:
            wait_bytes(hop_sent.at[step], hop_send_sem.at[step])
    wait_bytes(w_in.at[core], wsend_sem.at[0])
    wait_bytes(w_out.at[core], wsend_sem.at[1])


def shards(up_state, down_state, entering, norm_gain, router, routes, w_in, w_out):
    tok, width = up_state.shape[1:]
    half_units = w_in.shape[1]
    chunks = width // CHUNK
    slots = CHIPS * CAP
    vmem = pl.BlockSpec(memory_space=pltpu.VMEM)
    hbm = pl.BlockSpec(memory_space=pl.ANY)
    dma = pltpu.SemaphoreType.DMA
    blocks = pltpu.VMEM((STEPS, chunks, slots, CHUNK), BF16)
    up_new, down_new = pl.pallas_call(
        window_kernel,
        name="relay_window",
        out_shape=(
            jax.ShapeDtypeStruct((tok, width), BF16),
            jax.ShapeDtypeStruct((tok, width), BF16),
        ),
        in_specs=[vmem] * 6 + [hbm] * 2,
        out_specs=(vmem, vmem),
        scratch_shapes=[
            pltpu.VMEM((2, width, half_units), BF16),
            pltpu.VMEM((2, half_units, width), BF16),
            pltpu.VMEM((STEPS, chunks, 2 * tok, CHUNK), BF16),
            blocks,
            blocks,
            blocks,
            blocks,
            pltpu.VMEM((STEPS - 1, chunks, 2 * tok, CHUNK), BF16),
            pltpu.VMEM((STEPS - 1, chunks, 2 * tok, CHUNK), BF16),
            pltpu.VMEM((2, slots // GROUPS, half_units), F32),
            pltpu.VMEM((2, slots // GROUPS, half_units), BF16),
            pltpu.VMEM((2 * STEPS, chunks, 8, CHUNK), BF16),
            dma((chunks,)),
            dma((chunks,)),
            dma((2,)),
            dma((STEPS,)),
            dma((STEPS, GROUPS, chunks)),
            dma((STEPS,)),
            dma((STEPS, GROUPS, chunks)),
            dma((STEPS - 1,)),
            dma((STEPS - 1, chunks)),
        ],
        compiler_params=pltpu.CompilerParams(
            collective_id=0, has_side_effects=True, vmem_limit_bytes=60 * 2**20
        ),
    )(
        up_state[0],
        down_state[0],
        entering,
        norm_gain,
        router[0],
        routes[0, :, 0],
        w_in,
        w_out,
    )
    return (up_new[None], down_new[None])


def solution(mesh):
    return jax.shard_map(
        shards,
        mesh=mesh,
        in_specs=(
            P("pipe", "expert", None),
            P("pipe", "expert", None),
            P(None, None, "expert", None),
            P("pipe", None),
            P("pipe", None, None),
            P("pipe", None, "expert", None, None),
            P(None, "expert"),
            P("expert", None),
        ),
        out_specs=(P("pipe", "expert", None), P("pipe", "expert", None)),
        check_vma=False,
    )
```

```python
import functools

import jax
import jax.numpy as jnp
from jax import lax
from jax.experimental import pallas as pl
from jax.experimental.pallas import tpu as pltpu
from jax.sharding import PartitionSpec as P

STEPS = 2
ROUTE_SCALE = 2.5
NORM_EPS = 1e-06

NX, NY = 4, 8
CHIPS = NX * NY
CAP = 4
CHUNK = 512
GROUPS = 2
LAG = 2
MESH = pl.DeviceIdType.MESH
BF16 = jnp.bfloat16
F32 = jnp.float32

OFFSETS = [(dx, dy) for dx in range(NX) for dy in range(NY)]


def hops(offset):
    return min(offset[0], NX - offset[0]) + min(offset[1], NY - offset[1])


def window_kernel(
    up_ref, down_ref, entering_ref, gain_ref, router_ref, routes_ref, w_in_ref, w_out_ref,
    up_out, down_out,
    start, entering, router, w_in, w_out, rows, sent, got, made, back, hop_sent, hop_got, acc, hidden, spare,
    in_sem, out_sem, wsend_sem, sent_sem, got_sem, made_sem, back_sem, hop_send_sem, hop_sem,
    load_sem,
):
    tok, width = up_ref.shape
    row_count = 2 * tok
    chunks = width // CHUNK
    slots = CHIPS * CAP
    group_rows = slots // GROUPS
    group_offsets = CHIPS // GROUPS

    section = lax.axis_index("pipe")
    last_section = lax.axis_size("pipe") - 1
    place = lax.axis_index("expert")
    core = place % 2
    chip_x = (place // 2) // NY
    chip_y = (place // 2) % NY
    partner = place + 1 - 2 * core
    above = lax.rem(section + 1, last_section + 1)
    below = lax.rem(section + last_section, last_section + 1)

    def peer(dx, dy, sign):
        x = (chip_x + sign * dx + NX) % NX
        y = (chip_y + sign * dy + NY) % NY
        return (x * NY + y) * 2 + core

    def columns(c):
        return pl.ds(pl.multiple_of(c * CHUNK, CHUNK), CHUNK)

    def local_weights(c, _):
        pltpu.make_async_copy(w_in_ref.at[columns(c)], w_in.at[core, columns(c)], in_sem.at[c]).start()
        pltpu.make_async_copy(
            w_out_ref.at[:, columns(c)], w_out.at[core, :, columns(c)], out_sem.at[c]
        ).start()
        return 0

    barrier = pltpu.get_barrier_semaphore()
    for dx, dy in sorted(OFFSETS[1:], key=hops, reverse=True):
        pl.semaphore_signal(
            barrier, inc=1, device_id={"expert": peer(dx, dy, 1)}, device_id_type=MESH
        )
    for target in (above, below):
        pl.semaphore_signal(barrier, inc=1, device_id={"pipe": target}, device_id_type=MESH)
    pl.semaphore_signal(barrier, inc=1, device_id={"expert": partner}, device_id_type=MESH)

    loads = [
        pltpu.make_async_copy(up_ref, start.at[pl.ds(0, tok)], load_sem.at[0]),
        pltpu.make_async_copy(down_ref, start.at[pl.ds(tok, tok)], load_sem.at[1]),
        pltpu.make_async_copy(router_ref, router, load_sem.at[2]),
        pltpu.make_async_copy(entering_ref, entering, load_sem.at[3]),
    ]
    for load in loads:
        load.start()
    lax.fori_loop(0, chunks, local_weights, 0)

    def route(step):
        ids = routes_ref[pl.ds(step, 1)]
        member = (ids == lax.broadcasted_iota(jnp.int32, (CHIPS, row_count), 0)).astype(F32)
        earlier = (
            lax.broadcasted_iota(jnp.int32, (row_count, row_count), 0)
            < lax.broadcasted_iota(jnp.int32, (row_count, row_count), 1)
        ).astype(F32)
        ranks = jnp.dot(member.astype(BF16), earlier.astype(BF16), preferred_element_type=F32)
        rank = jnp.sum(ranks * member, axis=0, keepdims=True).astype(jnp.int32)
        far_x = (lax.div(ids, NY) - chip_x + NX) & (NX - 1)
        far_y = ((ids & (NY - 1)) - chip_y + NY) & (NY - 1)
        slot = (far_x * NY + far_y) * CAP + rank
        holds = (slot == lax.broadcasted_iota(jnp.int32, (slots, row_count), 0)).astype(F32)
        return jnp.transpose(member), jnp.transpose(holds).astype(BF16), holds.astype(BF16)

    plans = [route(step) for step in range(STEPS)]

    def admit(step, c, carry, chunk_rows):
        square, scores = carry
        rows[step, c] = chunk_rows
        values = chunk_rows.astype(F32)
        square = square + jnp.sum(values * values, axis=1, keepdims=True)
        scaled = (values * gain_ref[:, columns(c)]).astype(BF16)
        scores = scores + lax.dot_general(
            scaled, router[:, columns(c)], (((1,), (1,)), ((), ())), preferred_element_type=F32
        )
        sent[step, c] = jnp.dot(plans[step][2], chunk_rows, preferred_element_type=F32).astype(BF16)
        return square, scores

    def dispatch(step, group, c):
        for k in range(group * group_offsets, (group + 1) * group_offsets):
            mine = sent.at[step, c, pl.ds(CAP * k, CAP)]
            theirs = got.at[step, c, pl.ds(CAP * k, CAP)]
            if k == 0:
                pltpu.make_async_copy(mine, theirs, got_sem.at[step, group, c]).start()
                pltpu.make_async_copy(
                    mine, spare.at[2 * step, c, pl.ds(0, CAP)], sent_sem.at[step]
                ).start()
                continue
            pltpu.make_async_remote_copy(
                src_ref=mine,
                dst_ref=theirs,
                send_sem=sent_sem.at[step],
                recv_sem=got_sem.at[step, group, c],
                device_id={"expert": peer(*OFFSETS[k], 1)},
                device_id_type=MESH,
            ).start()

    def give_back(step, group, c):
        for k in range(group * group_offsets, (group + 1) * group_offsets):
            mine = made.at[step, c, pl.ds(CAP * k, CAP)]
            theirs = back.at[step, c, pl.ds(CAP * k, CAP)]
            if k == 0:
                pltpu.make_async_copy(mine, theirs, back_sem.at[step, group, c]).start()
                pltpu.make_async_copy(
                    mine, spare.at[2 * step + 1, c, pl.ds(0, CAP)], made_sem.at[step]
                ).start()
                continue
            pltpu.make_async_remote_copy(
                src_ref=mine,
                dst_ref=theirs,
                send_sem=made_sem.at[step],
                recv_sem=back_sem.at[step, group, c],
                device_id={"expert": peer(*OFFSETS[k], -1)},
                device_id_type=MESH,
            ).start()

    def wait_bytes(ref, sem):
        pltpu.make_async_copy(ref, ref, sem).wait()

    def experts(step, group):
        own = pl.ds(group * group_rows, group_rows)
        acc[...] = jnp.zeros_like(acc)

        def enter(c, square):
            wait_bytes(got.at[step, c, own], got_sem.at[step, group, c])
            if step == 0 and group == 0:
                wait_bytes(w_in.at[:, columns(c)], in_sem.at[c])
            values = got[step, c, own].astype(F32)
            square = square + jnp.sum(values * values, axis=1, keepdims=True)
            scaled = (values * gain_ref[:, columns(c)]).astype(BF16)
            for half in range(2):
                acc[half] += jnp.dot(scaled, w_in[half, columns(c)], preferred_element_type=F32)
            return square

        square = lax.fori_loop(0, chunks, enter, jnp.zeros((group_rows, 1), F32))
        factor = lax.rsqrt(square * (1.0 / width) + NORM_EPS)
        for half in range(2):
            hidden[half] = jax.nn.silu(acc[half] * factor).astype(BF16)

        def leave(c, _):
            if step == 0 and group == 0:
                wait_bytes(w_out.at[:, :, columns(c)], out_sem.at[c])
            total = jnp.dot(hidden[0], w_out[0, :, columns(c)], preferred_element_type=F32)
            total += jnp.dot(hidden[1], w_out[1, :, columns(c)], preferred_element_type=F32)
            made[step, c, own] = total.astype(BF16)
            give_back(step, group, c)
            return 0

        lax.fori_loop(0, chunks, leave, 0)

    def gate_of(step, carry):
        square, scores = carry
        factor = lax.rsqrt(square * (1.0 / width) + NORM_EPS)
        weights = jax.nn.sigmoid(scores * factor)
        return ROUTE_SCALE * jnp.sum(weights * plans[step][0], axis=1, keepdims=True)

    def combine(step, c, gate):
        for group in range(GROUPS):
            own = pl.ds(group * group_rows, group_rows)
            wait_bytes(back.at[step, c, own], back_sem.at[step, group, c])
        chosen = jnp.dot(plans[step][1], back[step, c], preferred_element_type=F32)
        return (rows[step, c].astype(F32) + gate * chosen).astype(BF16)

    empty = (jnp.zeros((row_count, 1), F32), jnp.zeros((row_count, CHIPS), F32))

    def first_rows(c, carry):
        return admit(0, c, carry, start[:, columns(c)])

    for load in loads[:3]:
        load.wait()
    carry = lax.fori_loop(0, chunks, first_rows, empty)

    pl.semaphore_wait(barrier, CHIPS + 2)

    def push_in(c, _):
        pltpu.make_async_remote_copy(
            src_ref=w_in_ref.at[columns(c)],
            dst_ref=w_in.at[core, columns(c)],
            send_sem=wsend_sem.at[0],
            recv_sem=in_sem.at[c],
            device_id={"expert": partner},
            device_id_type=MESH,
        ).start()
        return 0

    def push_out(c, _):
        pltpu.make_async_remote_copy(
            src_ref=w_out_ref.at[:, columns(c)],
            dst_ref=w_out.at[core, :, columns(c)],
            send_sem=wsend_sem.at[1],
            recv_sem=out_sem.at[c],
            device_id={"expert": partner},
            device_id_type=MESH,
        ).start()
        return 0

    def send_group(step, group):
        def one(c, _):
            dispatch(step, group, c)
            return 0

        lax.fori_loop(0, chunks, one, 0)

    send_group(0, 0)
    lax.fori_loop(0, chunks, push_in, 0)
    for group in range(1, GROUPS):
        send_group(0, group)
    lax.fori_loop(0, chunks, push_out, 0)

    for step in range(STEPS):
        gate = gate_of(step, carry)
        for group in range(GROUPS):
            experts(step, group)
        if step + 1 < STEPS:
            if step == 0:
                loads[3].wait()

            def relay(c):
                hop_sent[step, c] = combine(step, c, gate)
                for half, target in ((0, above), (1, below)):
                    part = pl.ds(half * tok, tok)
                    pltpu.make_async_remote_copy(
                        src_ref=hop_sent.at[step, c, part],
                        dst_ref=hop_got.at[step, c, part],
                        send_sem=hop_send_sem.at[step],
                        recv_sem=hop_sem.at[step, c],
                        device_id={"pipe": target},
                        device_id_type=MESH,
                    ).start()

            def take(c, carry):
                wait_bytes(hop_got.at[step, c], hop_sem.at[step, c])
                upward = jnp.where(
                    section == 0, entering[0, step, :, columns(c)], hop_got[step, c, pl.ds(0, tok)]
                )
                downward = jnp.where(
                    section == last_section,
                    entering[1, step, :, columns(c)],
                    hop_got[step, c, pl.ds(tok, tok)],
                )
                carry = admit(step + 1, c, carry, jnp.concatenate([upward, downward], axis=0))
                dispatch(step + 1, 0, c)
                return carry

            def head(c, _):
                relay(c)
                return 0

            def middle(c, carry):
                relay(c)
                return take(c - LAG, carry)

            lax.fori_loop(0, LAG, head, 0)
            carry = lax.fori_loop(LAG, chunks, middle, empty)
            carry = lax.fori_loop(chunks - LAG, chunks, take, carry)
            for group in range(1, GROUPS):
                send_group(step + 1, group)
        else:

            def finish(c, _):
                result = combine(step, c, gate)
                up_out[:, columns(c)] = result[:tok]
                down_out[:, columns(c)] = result[tok:]
                return 0

            lax.fori_loop(0, chunks, finish, 0)

    for step in range(STEPS):
        wait_bytes(sent.at[step], sent_sem.at[step])
        wait_bytes(made.at[step], made_sem.at[step])
        if step + 1 < STEPS:
            wait_bytes(hop_sent.at[step], hop_send_sem.at[step])
    wait_bytes(w_in.at[core], wsend_sem.at[0])
    wait_bytes(w_out.at[core], wsend_sem.at[1])


def hand_over(up_ref, down_ref, up_out, down_out):
    up_out[...] = up_ref[...]
    down_out[...] = down_ref[...]


def shards(up_state, down_state, entering, norm_gain, router, routes, w_in, w_out):
    tok, width = up_state.shape[1:]
    half_units = w_in.shape[1]
    chunks = width // CHUNK
    slots = CHIPS * CAP
    vmem = pl.BlockSpec(memory_space=pltpu.VMEM)
    hbm = pl.BlockSpec(memory_space=pltpu.HBM)
    dma = pltpu.SemaphoreType.DMA
    blocks = pltpu.VMEM((STEPS, chunks, slots, CHUNK), BF16)
    up_new, down_new = pl.pallas_call(
        window_kernel,
        name="relay_window",
        out_shape=(
            jax.ShapeDtypeStruct((tok, width), BF16),
            jax.ShapeDtypeStruct((tok, width), BF16),
        ),
        in_specs=[hbm] * 3 + [vmem, hbm, vmem] + [hbm] * 2,
        out_specs=(vmem, vmem),
        scratch_shapes=[
            pltpu.VMEM((2 * tok, width), BF16),
            pltpu.VMEM(entering.shape, BF16),
            pltpu.VMEM((CHIPS, width), BF16),
            pltpu.VMEM((2, width, half_units), BF16),
            pltpu.VMEM((2, half_units, width), BF16),
            pltpu.VMEM((STEPS, chunks, 2 * tok, CHUNK), BF16),
            blocks,
            blocks,
            blocks,
            blocks,
            pltpu.VMEM((STEPS - 1, chunks, 2 * tok, CHUNK), BF16),
            pltpu.VMEM((STEPS - 1, chunks, 2 * tok, CHUNK), BF16),
            pltpu.VMEM((2, slots // GROUPS, half_units), F32),
            pltpu.VMEM((2, slots // GROUPS, half_units), BF16),
            pltpu.VMEM((2 * STEPS, chunks, 8, CHUNK), BF16),
            dma((chunks,)),
            dma((chunks,)),
            dma((2,)),
            dma((STEPS,)),
            dma((STEPS, GROUPS, chunks)),
            dma((STEPS,)),
            dma((STEPS, GROUPS, chunks)),
            dma((STEPS - 1,)),
            dma((STEPS - 1, chunks)),
            dma((4,)),
        ],
        compiler_params=pltpu.CompilerParams(
            collective_id=0, has_side_effects=True, vmem_limit_bytes=60 * 2**20
        ),
    )(
        up_state[0],
        down_state[0],
        entering,
        norm_gain,
        router[0].T,
        routes[0, :, 0, :, 0],
        w_in,
        w_out,
    )
    result = jax.ShapeDtypeStruct((tok, width), BF16)
    up_new, down_new = pl.pallas_call(
        hand_over,
        name="hand_over",
        out_shape=(result, result),
        in_specs=[vmem, vmem],
        out_specs=(vmem, vmem),
    )(up_new, down_new)
    return (up_new[None], down_new[None])


def solution(mesh):
    return jax.shard_map(
        shards,
        mesh=mesh,
        in_specs=(
            P("pipe", "expert", None),
            P("pipe", "expert", None),
            P(None, None, "expert", None),
            P("pipe", None),
            P("pipe", None, None),
            P("pipe", None, "expert", None, None),
            P(None, "expert"),
            P("expert", None),
        ),
        out_specs=(P("pipe", "expert", None), P("pipe", "expert", None)),
        check_vma=False,
    )
```

```python
import functools

import jax
import jax.numpy as jnp
from jax import lax
from jax.experimental import pallas as pl
from jax.experimental.pallas import tpu as pltpu
from jax.sharding import PartitionSpec as P

STEPS = 2
ROUTE_SCALE = 2.5
NORM_EPS = 1e-06

NX, NY = 4, 8
CHIPS = NX * NY
CAP = 4
CHUNK = 512
GROUPS = 2
LAG = 2
MESH = pl.DeviceIdType.MESH
BF16 = jnp.bfloat16
F32 = jnp.float32

OFFSETS = [(dx, dy) for dx in range(NX) for dy in range(NY)]


def hops(offset):
    return min(offset[0], NX - offset[0]) + min(offset[1], NY - offset[1])


def window_kernel(
    up_ref, down_ref, entering_ref, gain_ref, router_ref, routes_ref, w_in_ref, w_out_ref,
    up_out, down_out,
    start, router, w_in, w_out, rows, sent, got, made, back, hop_sent, hop_got, acc, hidden, spare,
    in_sem, out_sem, wsend_sem, sent_sem, got_sem, made_sem, back_sem, hop_send_sem, hop_sem,
    load_sem,
):
    tok, width = up_ref.shape
    row_count = 2 * tok
    chunks = width // CHUNK
    slots = CHIPS * CAP
    group_rows = slots // GROUPS
    group_offsets = CHIPS // GROUPS

    section = lax.axis_index("pipe")
    last_section = lax.axis_size("pipe") - 1
    place = lax.axis_index("expert")
    core = place % 2
    chip_x = (place // 2) // NY
    chip_y = (place // 2) % NY
    partner = place + 1 - 2 * core
    above = section + 1
    below = section - 1
    neighbours = (section + last_section) // (last_section + 1) + (
        2 * last_section - section
    ) // (last_section + 1)

    def peer(dx, dy, sign):
        x = (chip_x + sign * dx + NX) % NX
        y = (chip_y + sign * dy + NY) % NY
        return (x * NY + y) * 2 + core

    def columns(c):
        return pl.ds(pl.multiple_of(c * CHUNK, CHUNK), CHUNK)

    def local_weights(c, _):
        pltpu.make_async_copy(w_in_ref.at[columns(c)], w_in.at[core, columns(c)], in_sem.at[c]).start()
        pltpu.make_async_copy(
            w_out_ref.at[:, columns(c)], w_out.at[core, :, columns(c)], out_sem.at[c]
        ).start()
        return 0

    barrier = pltpu.get_barrier_semaphore()
    for dx, dy in sorted(OFFSETS[1:], key=hops, reverse=True):
        pl.semaphore_signal(
            barrier, inc=1, device_id={"expert": peer(dx, dy, 1)}, device_id_type=MESH
        )
    for inside, target in ((section < last_section, above), (section > 0, below)):

        @pl.when(inside)
        def _(target=target):
            pl.semaphore_signal(barrier, inc=1, device_id={"pipe": target}, device_id_type=MESH)

    pl.semaphore_signal(barrier, inc=1, device_id={"expert": partner}, device_id_type=MESH)

    loads = [
        pltpu.make_async_copy(up_ref, start.at[pl.ds(0, tok)], load_sem.at[0]),
        pltpu.make_async_copy(down_ref, start.at[pl.ds(tok, tok)], load_sem.at[1]),
        pltpu.make_async_copy(router_ref, router, load_sem.at[2]),
    ]
    for load in loads:
        load.start()
    lax.fori_loop(0, chunks, local_weights, 0)

    for side, at_edge in ((0, section == 0), (1, section == last_section)):

        @pl.when(at_edge)
        def _(side=side):
            for step in range(STEPS - 1):

                def enter_edge(c, _):
                    pltpu.make_async_copy(
                        entering_ref.at[side, step, :, columns(c)],
                        hop_got.at[step, c, pl.ds(side * tok, tok)],
                        hop_sem.at[step, c],
                    ).start()
                    return 0

                lax.fori_loop(0, chunks, enter_edge, 0)

    def route(step):
        ids = routes_ref[pl.ds(step, 1)]
        member = (ids == lax.broadcasted_iota(jnp.int32, (CHIPS, row_count), 0)).astype(F32)
        earlier = (
            lax.broadcasted_iota(jnp.int32, (row_count, row_count), 0)
            < lax.broadcasted_iota(jnp.int32, (row_count, row_count), 1)
        ).astype(F32)
        ranks = jnp.dot(member.astype(BF16), earlier.astype(BF16), preferred_element_type=F32)
        rank = jnp.sum(ranks * member, axis=0, keepdims=True).astype(jnp.int32)
        far_x = (lax.div(ids, NY) - chip_x + NX) & (NX - 1)
        far_y = ((ids & (NY - 1)) - chip_y + NY) & (NY - 1)
        slot = (far_x * NY + far_y) * CAP + rank
        holds = (slot == lax.broadcasted_iota(jnp.int32, (slots, row_count), 0)).astype(F32)
        return jnp.transpose(member), jnp.transpose(holds).astype(BF16), holds.astype(BF16)

    plans = [route(step) for step in range(STEPS)]

    def admit(step, c, carry, chunk_rows):
        square, scores = carry
        rows[step, c] = chunk_rows
        values = chunk_rows.astype(F32)
        square = square + jnp.sum(values * values, axis=1, keepdims=True)
        scaled = (values * gain_ref[:, columns(c)]).astype(BF16)
        scores = scores + lax.dot_general(
            scaled, router[:, columns(c)], (((1,), (1,)), ((), ())), preferred_element_type=F32
        )
        sent[step, c] = jnp.dot(plans[step][2], chunk_rows, preferred_element_type=F32).astype(BF16)
        return square, scores

    def dispatch(step, group, c):
        for k in range(group * group_offsets, (group + 1) * group_offsets):
            mine = sent.at[step, c, pl.ds(CAP * k, CAP)]
            theirs = got.at[step, c, pl.ds(CAP * k, CAP)]
            if k == 0:
                pltpu.make_async_copy(mine, theirs, got_sem.at[step, group, c]).start()
                pltpu.make_async_copy(
                    mine, spare.at[2 * step, c, pl.ds(0, CAP)], sent_sem.at[step]
                ).start()
                continue
            pltpu.make_async_remote_copy(
                src_ref=mine,
                dst_ref=theirs,
                send_sem=sent_sem.at[step],
                recv_sem=got_sem.at[step, group, c],
                device_id={"expert": peer(*OFFSETS[k], 1)},
                device_id_type=MESH,
            ).start()

    def give_back(step, group, c):
        for k in range(group * group_offsets, (group + 1) * group_offsets):
            mine = made.at[step, c, pl.ds(CAP * k, CAP)]
            theirs = back.at[step, c, pl.ds(CAP * k, CAP)]
            if k == 0:
                pltpu.make_async_copy(mine, theirs, back_sem.at[step, group, c]).start()
                pltpu.make_async_copy(
                    mine, spare.at[2 * step + 1, c, pl.ds(0, CAP)], made_sem.at[step]
                ).start()
                continue
            pltpu.make_async_remote_copy(
                src_ref=mine,
                dst_ref=theirs,
                send_sem=made_sem.at[step],
                recv_sem=back_sem.at[step, group, c],
                device_id={"expert": peer(*OFFSETS[k], -1)},
                device_id_type=MESH,
            ).start()

    def wait_bytes(ref, sem):
        pltpu.make_async_copy(ref, ref, sem).wait()

    def experts(step, group):
        own = pl.ds(group * group_rows, group_rows)
        acc[...] = jnp.zeros_like(acc)

        def enter(c, square):
            wait_bytes(got.at[step, c, own], got_sem.at[step, group, c])
            if step == 0 and group == 0:
                wait_bytes(w_in.at[:, columns(c)], in_sem.at[c])
            values = got[step, c, own].astype(F32)
            square = square + jnp.sum(values * values, axis=1, keepdims=True)
            scaled = (values * gain_ref[:, columns(c)]).astype(BF16)
            for half in range(2):
                acc[half] += jnp.dot(scaled, w_in[half, columns(c)], preferred_element_type=F32)
            return square

        square = lax.fori_loop(0, chunks, enter, jnp.zeros((group_rows, 1), F32))
        factor = lax.rsqrt(square * (1.0 / width) + NORM_EPS)
        for half in range(2):
            hidden[half] = jax.nn.silu(acc[half] * factor).astype(BF16)

        def leave(c, _):
            if step == 0 and group == 0:
                wait_bytes(w_out.at[:, :, columns(c)], out_sem.at[c])
            total = jnp.dot(hidden[0], w_out[0, :, columns(c)], preferred_element_type=F32)
            total += jnp.dot(hidden[1], w_out[1, :, columns(c)], preferred_element_type=F32)
            made[step, c, own] = total.astype(BF16)
            give_back(step, group, c)
            return 0

        lax.fori_loop(0, chunks, leave, 0)

    def gate_of(step, carry):
        square, scores = carry
        factor = lax.rsqrt(square * (1.0 / width) + NORM_EPS)
        weights = jax.nn.sigmoid(scores * factor)
        return ROUTE_SCALE * jnp.sum(weights * plans[step][0], axis=1, keepdims=True)

    def combine(step, c, gate):
        for group in range(GROUPS):
            own = pl.ds(group * group_rows, group_rows)
            wait_bytes(back.at[step, c, own], back_sem.at[step, group, c])
        chosen = jnp.dot(plans[step][1], back[step, c], preferred_element_type=F32)
        return (rows[step, c].astype(F32) + gate * chosen).astype(BF16)

    empty = (jnp.zeros((row_count, 1), F32), jnp.zeros((row_count, CHIPS), F32))

    def first_rows(c, carry):
        return admit(0, c, carry, start[:, columns(c)])

    for load in loads:
        load.wait()
    carry = lax.fori_loop(0, chunks, first_rows, empty)

    pl.semaphore_wait(barrier, CHIPS + neighbours)

    def push_in(c, _):
        pltpu.make_async_remote_copy(
            src_ref=w_in_ref.at[columns(c)],
            dst_ref=w_in.at[core, columns(c)],
            send_sem=wsend_sem.at[0],
            recv_sem=in_sem.at[c],
            device_id={"expert": partner},
            device_id_type=MESH,
        ).start()
        return 0

    def push_out(c, _):
        pltpu.make_async_remote_copy(
            src_ref=w_out_ref.at[:, columns(c)],
            dst_ref=w_out.at[core, :, columns(c)],
            send_sem=wsend_sem.at[1],
            recv_sem=out_sem.at[c],
            device_id={"expert": partner},
            device_id_type=MESH,
        ).start()
        return 0

    def send_group(step, group):
        def one(c, _):
            dispatch(step, group, c)
            return 0

        lax.fori_loop(0, chunks, one, 0)

    send_group(0, 0)
    lax.fori_loop(0, chunks, push_in, 0)
    for group in range(1, GROUPS):
        send_group(0, group)
    lax.fori_loop(0, chunks, push_out, 0)

    for step in range(STEPS):
        gate = gate_of(step, carry)
        for group in range(GROUPS):
            experts(step, group)
        if step + 1 < STEPS:

            def relay(c):
                hop_sent[step, c] = combine(step, c, gate)
                for half, inside, target in (
                    (0, section < last_section, above),
                    (1, section > 0, below),
                ):

                    @pl.when(inside)
                    def _(half=half, target=target):
                        part = pl.ds(half * tok, tok)
                        pltpu.make_async_remote_copy(
                            src_ref=hop_sent.at[step, c, part],
                            dst_ref=hop_got.at[step, c, part],
                            send_sem=hop_send_sem.at[step, half],
                            recv_sem=hop_sem.at[step, c],
                            device_id={"pipe": target},
                            device_id_type=MESH,
                        ).start()


            def take(c, carry):
                wait_bytes(hop_got.at[step, c], hop_sem.at[step, c])
                carry = admit(step + 1, c, carry, hop_got[step, c])
                dispatch(step + 1, 0, c)
                return carry

            def head(c, _):
                relay(c)
                return 0

            def middle(c, carry):
                relay(c)
                return take(c - LAG, carry)

            lax.fori_loop(0, LAG, head, 0)
            carry = lax.fori_loop(LAG, chunks, middle, empty)
            carry = lax.fori_loop(chunks - LAG, chunks, take, carry)
            for group in range(1, GROUPS):
                send_group(step + 1, group)
        else:

            def finish(c, _):
                result = combine(step, c, gate)
                up_out[:, columns(c)] = result[:tok]
                down_out[:, columns(c)] = result[tok:]
                return 0

            lax.fori_loop(0, chunks, finish, 0)

    for step in range(STEPS):
        wait_bytes(sent.at[step], sent_sem.at[step])
        wait_bytes(made.at[step], made_sem.at[step])
        if step + 1 < STEPS:
            for half, inside in ((0, section < last_section), (1, section > 0)):

                @pl.when(inside)
                def _(step=step, half=half):
                    part = pl.ds(half * tok, tok)
                    wait_bytes(hop_sent.at[step, :, part], hop_send_sem.at[step, half])

    wait_bytes(w_in.at[core], wsend_sem.at[0])
    wait_bytes(w_out.at[core], wsend_sem.at[1])


def hand_over(up_ref, down_ref, up_out, down_out):
    up_out[...] = up_ref[...]
    down_out[...] = down_ref[...]


def shards(up_state, down_state, entering, norm_gain, router, routes, w_in, w_out):
    tok, width = up_state.shape[1:]
    half_units = w_in.shape[1]
    chunks = width // CHUNK
    slots = CHIPS * CAP
    vmem = pl.BlockSpec(memory_space=pltpu.VMEM)
    hbm = pl.BlockSpec(memory_space=pltpu.HBM)
    dma = pltpu.SemaphoreType.DMA
    blocks = pltpu.VMEM((STEPS, chunks, slots, CHUNK), BF16)
    up_new, down_new = pl.pallas_call(
        window_kernel,
        name="relay_window",
        out_shape=(
            jax.ShapeDtypeStruct((tok, width), BF16),
            jax.ShapeDtypeStruct((tok, width), BF16),
        ),
        in_specs=[hbm] * 3 + [vmem, hbm, vmem] + [hbm] * 2,
        out_specs=(vmem, vmem),
        scratch_shapes=[
            pltpu.VMEM((2 * tok, width), BF16),
            pltpu.VMEM((CHIPS, width), BF16),
            pltpu.VMEM((2, width, half_units), BF16),
            pltpu.VMEM((2, half_units, width), BF16),
            pltpu.VMEM((STEPS, chunks, 2 * tok, CHUNK), BF16),
            blocks,
            blocks,
            blocks,
            blocks,
            pltpu.VMEM((STEPS - 1, chunks, 2 * tok, CHUNK), BF16),
            pltpu.VMEM((STEPS - 1, chunks, 2 * tok, CHUNK), BF16),
            pltpu.VMEM((2, slots // GROUPS, half_units), F32),
            pltpu.VMEM((2, slots // GROUPS, half_units), BF16),
            pltpu.VMEM((2 * STEPS, chunks, 8, CHUNK), BF16),
            dma((chunks,)),
            dma((chunks,)),
            dma((2,)),
            dma((STEPS,)),
            dma((STEPS, GROUPS, chunks)),
            dma((STEPS,)),
            dma((STEPS, GROUPS, chunks)),
            dma((STEPS - 1, 2)),
            dma((STEPS - 1, chunks)),
            dma((3,)),
        ],
        compiler_params=pltpu.CompilerParams(
            collective_id=0, has_side_effects=True, vmem_limit_bytes=60 * 2**20
        ),
    )(
        up_state[0],
        down_state[0],
        entering,
        norm_gain,
        router[0].T,
        routes[0, :, 0, :, 0],
        w_in,
        w_out,
    )
    result = jax.ShapeDtypeStruct((tok, width), BF16)
    up_new, down_new = pl.pallas_call(
        hand_over,
        name="hand_over",
        out_shape=(result, result),
        in_specs=[vmem, vmem],
        out_specs=(vmem, vmem),
    )(up_new, down_new)
    return (up_new[None], down_new[None])


def solution(mesh):
    return jax.shard_map(
        shards,
        mesh=mesh,
        in_specs=(
            P("pipe", "expert", None),
            P("pipe", "expert", None),
            P(None, None, "expert", None),
            P("pipe", None),
            P("pipe", None, None),
            P("pipe", None, "expert", None, None),
            P(None, "expert"),
            P("expert", None),
        ),
        out_specs=(P("pipe", "expert", None), P("pipe", "expert", None)),
        check_vma=False,
    )
```
